32 devices in a mesh: gx: 8 (over z, y), gy: 4 (over x, core).
Axes of the slice: x: 2, y: 2, z: 4, core: 2. Of those that a mesh axis runs over, the one named last changes fastest.
Arguments:
- fields: float32 [4, 2048, 16, 2048], P(None, 'gx', None, 'gy'), may hold values from -6 to 6
- slope_x: float32 [2048, 2048], P('gx', 'gy'), may hold values from -0.5 to 0.5
- slope_y: float32 [2048, 2048], P('gx', 'gy'), may hold values from -0.5 to 0.5
- fringe_mask: int32 [2048], P('gx'), may hold values 0 or 1
- plane_x: int32 [1], replicated, may hold values from 0 to 2047
- joint_bin: int32 [2048, 16, 2048], P('gx', None, 'gy'), may hold values from 0 to 4095
Outputs:
- tendency: float32 [4, 2048, 16, 2048], P(None, 'gx', None, 'gy')
- histogram: float32 [64, 64], P('gx', 'gy')
The draws below stay inside these ranges and needn't reach their ends.
All inputs are finite; a program needn't handle non-finite values. No bound on the sum of `fringe_mask` on one device may be relied on, other than what follows from the above.
Results may differ from the reference program's by a relative error of at most 0.0004.
Values sent between devices are 32-bit elements; how exact they have to be, the bound alone decides.
No kernel may reach another device: no remote copies, remote signals or barrier semaphores. Data moves between devices by JAX's collectives and lax.ppermute only.
A program may use at most 384 MiB of HBM per device.

```python
import jax
import jax.numpy as jnp
from jax import lax

NX = 2048
LZ = 16
LEVELS = 384
BINS = 64
NY = 2048


def set_ends(result, rng, low, top_value):
    spot = [jax.random.randint(jax.random.fold_in(rng, axis), (), 0, length) for axis, length in enumerate(result.shape)]
    widest = result.shape.index(max(result.shape))
    beside = spot[:widest] + [(spot[widest] + 1) % result.shape[widest]] + spot[widest + 1:]
    return result.at[tuple(spot)].set(low).at[tuple(beside)].set(top_value)


def steps_of(stream_key, dims, split, low, high):
    level, own = 1.0, jax.random.fold_in(stream_key, 6)
    for axis_at, parts in split:
        heights = jnp.exp(jax.random.uniform(jax.random.fold_in(own, axis_at), (parts,), jnp.float32, low / len(split), high / len(split)))
        level = level * jnp.repeat(heights, dims[axis_at] // parts).reshape([-1 if axis == axis_at else 1 for axis in range(len(dims))])
    return level


def noise(own_key, extent, deviation, reach, split=(), kind=jnp.bfloat16):
    entries = deviation * jax.random.normal(own_key, extent, jnp.float32)
    if split:
        entries = entries * steps_of(own_key, extent, split, -0.22, 0.18)
    return jnp.clip(entries, -reach, reach).astype(kind)


def setup_inputs(seed: int = 0) -> dict:
    key_list = jax.random.split(jax.random.key(seed), 7)
    return {
        "fields": noise(key_list[0], (4, NX, LZ, NY), 1.0, 6.0, ((1, 8), (3, 4)), jnp.float32),
        "slope_x": jnp.clip(jax.random.uniform(key_list[1], (NX, NY), jnp.float32, -0.5, 0.5) * steps_of(key_list[1], (NX, NY), ((0, 8), (1, 4)), -0.4, 0.0), -0.5, 0.5),
        "slope_y": jnp.clip(jax.random.uniform(key_list[2], (NX, NY), jnp.float32, -0.5, 0.5) * steps_of(key_list[2], (NX, NY), ((0, 8), (1, 4)), -0.4, 0.0), -0.5, 0.5),
        "fringe_mask": set_ends((jax.random.randint(key_list[3], (NX,), 0, 4) < 1).astype(jnp.int32), jax.random.fold_in(key_list[3], 1), 0, 1),
        "plane_x": jax.random.randint(key_list[4], (1,), 0, NX).astype(jnp.int32),
        "joint_bin": set_ends(jax.random.randint(key_list[5], (NX, LZ, NY), 0, BINS * BINS), jax.random.fold_in(key_list[5], 1), 0, (BINS * BINS) - 1).astype(jnp.int32),
    }


FRINGE_RATE = 0.5
BUOYANCY = 0.5
SECTION_DT = 0.25


def level_derivative(field):
    levels = field.shape[-2]
    upper = jnp.concatenate([field[..., 1:, :], field[..., -1:, :]], axis=-2)
    lower = jnp.concatenate([field[..., :1, :], field[..., :-1, :]], axis=-2)
    position = jnp.arange(levels, dtype=jnp.int32)
    spacing = jnp.where((position == 0) | (position == levels - 1), 1.0, 2.0).astype(field.dtype)
    return (upper - lower) / spacing[:, None]


def stream_derivative(field):
    count = field.shape[0]
    spectrum = jnp.fft.rfft(field, axis=0)
    modes = jnp.arange(count // 2 + 1, dtype=jnp.int32)
    wave = 2.0 * jnp.pi * modes.astype(field.dtype) / count
    wave = jnp.where(modes == count // 2, 0.0, wave).astype(field.dtype)
    return jnp.fft.irfft(spectrum * (1j * wave)[:, None, None], n=count, axis=0).astype(field.dtype)


def span_derivative(field):
    ahead_one = jnp.roll(field, -1, axis=-1)
    behind_one = jnp.roll(field, 1, axis=-1)
    ahead_two = jnp.roll(field, -2, axis=-1)
    behind_two = jnp.roll(field, 2, axis=-1)
    return (8.0 * (ahead_one - behind_one) - (ahead_two - behind_two)) / 12.0


def reference(fields, slope_x, slope_y, fringe_mask, plane_x, joint_bin):
    level_pos = (jnp.arange(LZ, dtype=jnp.int32).astype(fields.dtype) + 0.5) / LEVELS
    shape_factor = (1.0 - level_pos)[None, :, None]
    metric_x = -slope_x[:, None, :] * shape_factor
    metric_y = -slope_y[:, None, :] * shape_factor
    level_slope = level_derivative(fields)
    stream_slope = lax.map(stream_derivative, fields)
    span_slope = span_derivative(fields)
    plane = lax.dynamic_index_in_dim(fields, plane_x[0], 1, keepdims=True)
    mask_float = fringe_mask.astype(fields.dtype)[:, None, None]
    tendency = (-fields[0] * (stream_slope + metric_x * level_slope)
                - fields[1] * (span_slope + metric_y * level_slope)
                - fields[2] * level_slope
                + FRINGE_RATE * mask_float * (plane - fields))
    tendency = tendency.at[2].add(BUOYANCY * fields[3])
    section = fields + SECTION_DT * tendency
    flux = (section[2] * section[3]).astype(jnp.bfloat16)
    sums = jax.ops.segment_sum(flux.astype(jnp.float32).reshape(-1), joint_bin.reshape(-1), num_segments=BINS * BINS)
    scale = (BINS * BINS / (NX * NY * LZ)) ** 0.5
    histogram = (sums * scale).reshape(BINS, BINS)
    return tendency, histogram
```

```python
import functools
import math

import jax
import jax.numpy as jnp
import ml_dtypes
import numpy as np
from jax import lax
from jax.experimental import pallas as pl
from jax.experimental.pallas import tpu as pltpu
from jax.sharding import PartitionSpec as P

LEVELS = 384
BINS = 64


FRINGE_RATE = 0.5
BUOYANCY = 0.5
SECTION_DT = 0.25

FACTOR_TOLERANCE = 1e-9


def broadcast(block, axis, owner):
    block = jnp.where(lax.axis_index(axis) == owner, block, jnp.zeros_like(block))
    return lax.psum(block, axis)


def padded(rank):
    return -(-rank // 8) * 8


def derivative_block(count, size, distance):
    table = np.zeros(count)
    for k in range(1, count):
        value = math.pi / count * math.cos(math.pi * k / count) / math.sin(math.pi * k / count)
        table[k] = round(value * 2.0**45) / 2.0**45 * (1 if k % 2 == 0 else -1)
    offset = np.arange(size)[:, None] - np.arange(size)[None, :] + distance * size
    return table[offset % count]


def factored(block, tolerance):
    rest = block.copy()
    left, right = [], []
    while True:
        row, col = np.unravel_index(np.argmax(np.abs(rest)), rest.shape)
        pivot = rest[row, col]
        if abs(pivot) <= tolerance and left:
            break
        left.append(rest[:, col] / pivot)
        right.append(rest[row, :].copy())
        rest = rest - left[-1][:, None] * right[-1][None, :]
    return np.stack(left, 1), np.stack(right, 0)


def pieces(matrix):
    rest, parts = matrix, []
    for _ in range(3):
        parts.append(rest.astype(ml_dtypes.bfloat16))
        rest = rest - parts[-1].astype(np.float64)
    high, middle, low = parts
    return np.concatenate([high, middle, low, high, middle, high], 1)


def operators(count, size):
    ranks, encode, decode = [], [], [derivative_block(count, size, 0)]
    for distance in range(1, count // size):
        left, right = factored(derivative_block(count, size, distance), FACTOR_TOLERANCE)
        rank = left.shape[1]
        ranks.append(rank)
        decode.append(np.pad(left, ((0, 0), (0, padded(rank) - rank))))
        encode.append(np.pad(right, ((0, padded(rank) - rank), (0, 0))))
    return pieces(np.concatenate(encode, 0)), pieces(np.concatenate(decode, 1)), tuple(ranks)


def split(value):
    high = value.astype(jnp.bfloat16)
    rest = value - high.astype(jnp.float32)
    middle = rest.astype(jnp.bfloat16)
    low = (rest - middle.astype(jnp.float32)).astype(jnp.bfloat16)
    return jnp.concatenate([high, high, high, middle, middle, low], 0)


def encode_kernel(matrix_ref, f_ref, *out_refs, levels, ranks):
    size = f_ref.shape[1] // levels

    def at_pair(pair, carry):
        parts = [
            f_ref[0, pl.ds(2 * pair + k, size, stride=levels), :] for k in range(2)
        ]
        coded = jnp.dot(
            matrix_ref[...],
            split(jnp.concatenate(parts, 1)),
            preferred_element_type=jnp.float32,
        )
        start = 0
        for rank, out_ref in zip(ranks, out_refs):
            for k in range(2):
                out_ref[0, pl.ds(2 * pair + k, rank, stride=levels), :] = coded[
                    start : start + rank, 128 * k : 128 * k + 128
                ]
            start += padded(rank)
        return carry

    lax.fori_loop(0, levels // 2, at_pair, 0, unroll=2)


def encoded(matrix, fields, ranks):
    count, size, levels, cols = fields.shape
    width = 128
    return pl.pallas_call(
        functools.partial(encode_kernel, levels=levels, ranks=ranks),
        grid=(count, cols // width),
        in_specs=[
            pl.BlockSpec(matrix.shape, lambda n, j: (0, 0)),
            pl.BlockSpec((1, size * levels, width), lambda n, j: (n, 0, j)),
        ],
        out_specs=[
            pl.BlockSpec((1, rank * levels, width), lambda n, j: (n, 0, j)) for rank in ranks
        ],
        out_shape=[
            jax.ShapeDtypeStruct((count, rank * levels, cols), jnp.float32) for rank in ranks
        ],
        compiler_params=pltpu.CompilerParams(vmem_limit_bytes=48 << 20),
    )(matrix, fields.reshape(count, size * levels, cols))


def decode_kernel(matrix_ref, f_ref, *refs, levels, ranks):
    code_refs, out_ref, scratch = refs[: len(ranks)], refs[-2], refs[-1]
    size = f_ref.shape[1] // levels
    scratch[...] = jnp.zeros_like(scratch)

    def at_pair(pair, carry):
        for k in range(2):
            lanes = slice(128 * k, 128 * k + 128)
            start = size
            scratch[:size, lanes] = f_ref[0, pl.ds(2 * pair + k, size, stride=levels), :]
            for rank, code_ref in zip(ranks, code_refs):
                scratch[start : start + rank, lanes] = code_ref[
                    0, pl.ds(2 * pair + k, rank, stride=levels), :
                ]
                start += padded(rank)
        slope = jnp.dot(
            matrix_ref[...], split(scratch[...]), preferred_element_type=jnp.float32
        )
        for k in range(2):
            out_ref[0, pl.ds(2 * pair + k, size, stride=levels), :] = slope[
                :, 128 * k : 128 * k + 128
            ]
        return carry

    lax.fori_loop(0, levels // 2, at_pair, 0)


def decoded(matrix, fields, codes, ranks):
    count, size, levels, cols = fields.shape
    width = 128
    total = size + sum(padded(rank) for rank in ranks)
    return pl.pallas_call(
        functools.partial(decode_kernel, levels=levels, ranks=ranks),
        grid=(count, cols // width),
        in_specs=[
            pl.BlockSpec(matrix.shape, lambda n, j: (0, 0)),
            pl.BlockSpec((1, size * levels, width), lambda n, j: (n, 0, j)),
        ]
        + [pl.BlockSpec((1, rank * levels, width), lambda n, j: (n, 0, j)) for rank in ranks],
        out_specs=pl.BlockSpec((1, size * levels, width), lambda n, j: (n, 0, j)),
        out_shape=jax.ShapeDtypeStruct((count, size * levels, cols), jnp.float32),
        scratch_shapes=[pltpu.VMEM((total, 2 * width), jnp.float32)],
        compiler_params=pltpu.CompilerParams(vmem_limit_bytes=48 << 20),
    )(matrix, fields.reshape(count, size * levels, cols), *codes).reshape(fields.shape)


def tendency_kernel(mask_ref, f_ref, halo_ref, s_ref, plane_ref, sx_ref, sy_ref, jb_ref, out_ref, hist_ref, *, rows):
    step = pl.program_id(0)
    levels, cols = f_ref.shape[2], f_ref.shape[3]

    @pl.when(step == 0)
    def _():
        hist_ref[...] = jnp.zeros_like(hist_ref)

    level = lax.broadcasted_iota(jnp.int32, (levels, cols), 0)
    shape_factor = 1.0 - (level.astype(jnp.float32) + 0.5) / LEVELS
    first = level == 0
    last = level == levels - 1
    inv = jnp.where(first | last, 1.0, 0.5)
    lane16 = lax.broadcasted_iota(jnp.int32, (16, cols), 0).astype(jnp.float32)
    iotas = [(lane16 + 16.0 * j).astype(jnp.bfloat16) for j in range(BINS // 16)]
    one = jnp.ones((16, cols), jnp.bfloat16)
    zero = jnp.zeros((16, cols), jnp.bfloat16)

    def row(x, carry):
        f = [f_ref[n, x] for n in range(4)]
        u, v, w, th = f
        sx = jnp.broadcast_to(sx_ref[pl.ds(x, 1), :], (levels, cols))
        sy = jnp.broadcast_to(sy_ref[pl.ds(x, 1), :], (levels, cols))
        across = w - shape_factor * (u * sx + v * sy)
        across = across * inv
        v12 = v * (1.0 / 12.0)
        rate = FRINGE_RATE * mask_ref[step * rows + x].astype(jnp.float32)
        tend = []
        for n in range(4):
            g = f[n]
            if True:
                up = jnp.where(last, g, pltpu.roll(g, levels - 1, 0))
                down = jnp.where(first, g, pltpu.roll(g, 1, 0))
                p = jnp.concatenate([g, halo_ref[n, x]], axis=1)
                width = cols + 128
                d1 = (pltpu.roll(p, width - 1, 1) - pltpu.roll(p, 1, 1))[:, :cols]
                d2 = (pltpu.roll(p, width - 2, 1) - pltpu.roll(p, 2, 1))[:, :cols]
                t = rate * (plane_ref[n] - g) - u * s_ref[n, x] - v12 * (8.0 * d1 - d2) - across * (up - down)
                if n == 2:
                    t = t + BUOYANCY * th
            out_ref[n, x] = t
            tend.append(t)
        flux = ((w + SECTION_DT * tend[2]) * (th + SECTION_DT * tend[3])).astype(jnp.bfloat16).astype(jnp.float32)
        jb = jb_ref[x]
        tb = (jb >> 6).astype(jnp.float32)
        wb = (jb & (BINS - 1)).astype(jnp.float32)
        lhs, rhs = [], []
        for q in range(levels // 4):
            lq, rq = [], []
            for l in range(4 * q, 4 * q + 4):
                tl = jnp.broadcast_to(tb[l:l + 1], (16, cols)).astype(jnp.bfloat16)
                wl = jnp.broadcast_to(wb[l:l + 1], (16, cols)).astype(jnp.bfloat16)
                fl = jnp.broadcast_to(flux[l:l + 1], (16, cols)).astype(jnp.bfloat16)
                lq += [jnp.where(tl == i, one, zero) for i in iotas]
                rq += [jnp.where(wl == i, fl, zero) for i in iotas]
            lhs.append(jnp.concatenate(lq, 0))
            rhs.append(jnp.concatenate(rq, 0))
        lhs = jnp.concatenate(lhs, 1)
        rhs = jnp.concatenate(rhs, 1)
        hist_ref[...] += lax.dot_general(lhs, rhs, (((1,), (1,)), ((), ())), preferred_element_type=jnp.float32)
        return carry

    lax.fori_loop(0, rows, row, 0)


def tendency_call(mask, fields, halo, stream, plane, slope_x, slope_y, jbin, rows=8):
    _, R, L, C = fields.shape
    big = pl.BlockSpec((4, rows, L, C), lambda i, m: (0, i, 0, 0))
    row2 = pl.BlockSpec((rows, C), lambda i, m: (i, 0))
    return pl.pallas_call(
        functools.partial(tendency_kernel, rows=rows),
        grid_spec=pltpu.PrefetchScalarGridSpec(
            num_scalar_prefetch=1, grid=(R // rows,),
            in_specs=[big, pl.BlockSpec((4, rows, L, 128), lambda i, m: (0, i, 0, 0)), big,
                      pl.BlockSpec((4, L, C), lambda i, m: (0, 0, 0)), row2, row2,
                      pl.BlockSpec((rows, L, C), lambda i, m: (i, 0, 0))],
            out_specs=[big, pl.BlockSpec((256, 256), lambda i, m: (0, 0))]),
        out_shape=[jax.ShapeDtypeStruct(fields.shape, jnp.float32), jax.ShapeDtypeStruct((256, 256), jnp.float32)],
        compiler_params=pltpu.CompilerParams(vmem_limit_bytes=56 << 20),
    )(mask, fields, halo, stream, plane, slope_x, slope_y, jbin)


def shards(fields, slope_x, slope_y, fringe_mask, plane_x, joint_bin):
    field_count, local_rows, levels, local_cols = fields.shape
    span, stream = lax.axis_size("gy"), lax.axis_size("gx")
    total_x, total_y = local_rows * stream, local_cols * span
    encoder, decoder, ranks = operators(total_x, local_rows)
    codes = encoded(encoder, fields, ranks)
    codes = [
        lax.ppermute(code, "gx", [(i, (i + distance) % stream) for i in range(stream)])
        for distance, code in enumerate(codes, 1)
    ]
    forward = [(i, (i + 1) % span) for i in range(span)]
    backward = [(target, source) for source, target in forward]
    low = lax.ppermute(fields[..., -2:], "gy", forward)
    high = lax.ppermute(fields[..., :2], "gy", backward)
    halo = jnp.concatenate([high, jnp.zeros(fields.shape[:3] + (124,), jnp.float32), low], -1)
    owner = plane_x[0] // local_rows
    own_row = lax.dynamic_index_in_dim(fields, plane_x[0] % local_rows, 1, keepdims=False)
    plane = broadcast(own_row, "gx", owner)
    stream_slope = decoded(decoder, fields, codes, ranks)
    tendency, square = tendency_call(
        fringe_mask, fields, halo, stream_slope, plane, slope_x, slope_y, joint_bin
    )
    sums = sum(square[BINS * i : BINS * i + BINS, BINS * i : BINS * i + BINS] for i in range(4))
    scale = (BINS * BINS / (total_x * total_y * levels)) ** 0.5
    combined = lax.psum(sums, ("gx", "gy"))
    row_share, col_share = BINS // stream, BINS // span
    own_sums = lax.dynamic_slice(
        combined,
        (lax.axis_index("gx") * row_share, lax.axis_index("gy") * col_share),
        (row_share, col_share),
    )
    return tendency, own_sums * scale


def solution(mesh):
    placed = (
        P(None, "gx", None, "gy"),
        P("gx", "gy"),
        P("gx", "gy"),
        P("gx"),
        P(),
        P("gx", None, "gy"),
    )
    return jax.shard_map(
        shards,
        mesh=mesh,
        in_specs=placed,
        out_specs=(P(None, "gx", None, "gy"), P("gx", "gy")),
        check_vma=False,
    )
```

```python
import functools
import math

import jax
import jax.numpy as jnp
import ml_dtypes
import numpy as np
from jax import lax
from jax.experimental import pallas as pl
from jax.experimental.pallas import tpu as pltpu
from jax.sharding import PartitionSpec as P

LEVELS = 384
BINS = 64


FRINGE_RATE = 0.5
BUOYANCY = 0.5
SECTION_DT = 0.25

FACTOR_TOLERANCE = 1e-9


def padded(rank):
    return -(-rank // 8) * 8


def derivative_block(count, size, distance):
    table = np.zeros(count)
    for k in range(1, count):
        value = math.pi / count * math.cos(math.pi * k / count) / math.sin(math.pi * k / count)
        table[k] = round(value * 2.0**45) / 2.0**45 * (1 if k % 2 == 0 else -1)
    offset = np.arange(size)[:, None] - np.arange(size)[None, :] + distance * size
    return table[offset % count]


def factored(block, tolerance):
    rest = block.copy()
    left, right = [], []
    while True:
        row, col = np.unravel_index(np.argmax(np.abs(rest)), rest.shape)
        pivot = rest[row, col]
        if abs(pivot) <= tolerance and left:
            break
        left.append(rest[:, col] / pivot)
        right.append(rest[row, :].copy())
        rest = rest - left[-1][:, None] * right[-1][None, :]
    return np.stack(left, 1), np.stack(right, 0)


def pieces(matrix):
    rest, parts = matrix, []
    for _ in range(3):
        parts.append(rest.astype(ml_dtypes.bfloat16))
        rest = rest - parts[-1].astype(np.float64)
    high, middle, low = parts
    return np.concatenate([high, middle, low, high, middle, high], 1)


def operators(count, size):
    ranks, encode, decode = [], [], [derivative_block(count, size, 0)]
    for distance in range(1, count // size):
        left, right = factored(derivative_block(count, size, distance), FACTOR_TOLERANCE)
        ranks.append(left.shape[1] + 1)
        spare = padded(ranks[-1]) - left.shape[1]
        decode.append(np.pad(left, ((0, 0), (0, spare))))
        encode.append(np.pad(right, ((0, spare), (0, 0))))
    return pieces(np.concatenate(encode, 0)), pieces(np.concatenate(decode, 1)), tuple(ranks)


def split(value):
    high = value.astype(jnp.bfloat16)
    rest = value - high.astype(jnp.float32)
    middle = rest.astype(jnp.bfloat16)
    low = (rest - middle.astype(jnp.float32)).astype(jnp.bfloat16)
    return jnp.concatenate([high, high, high, middle, middle, low], 0)


def encode_kernel(matrix_ref, f_ref, *out_refs, levels, ranks):
    size = f_ref.shape[1] // levels

    def at_pair(pair, carry):
        parts = [
            f_ref[0, pl.ds(2 * pair + k, size, stride=levels), :] for k in range(2)
        ]
        coded = jnp.dot(
            matrix_ref[...],
            split(jnp.concatenate(parts, 1)),
            preferred_element_type=jnp.float32,
        )
        start = 0
        for rank, out_ref in zip(ranks, out_refs):
            for k in range(2):
                out_ref[0, pl.ds(2 * pair + k, rank, stride=levels), :] = coded[
                    start : start + rank, 128 * k : 128 * k + 128
                ]
            start += padded(rank)
        return carry

    lax.fori_loop(0, levels // 2, at_pair, 0, unroll=4)


def encoded(matrix, fields, ranks, first, tiles):
    count, size, levels, _ = fields.shape
    width = 128
    cols = tiles * width
    return pl.pallas_call(
        functools.partial(encode_kernel, levels=levels, ranks=ranks),
        grid=(count, cols // width),
        in_specs=[
            pl.BlockSpec(matrix.shape, lambda n, j: (0, 0)),
            pl.BlockSpec((1, size * levels, width), lambda n, j: (n, 0, first + j)),
        ],
        out_specs=[
            pl.BlockSpec((1, rank * levels, width), lambda n, j: (n, 0, j)) for rank in ranks
        ],
        out_shape=[
            jax.ShapeDtypeStruct((count, rank * levels, cols), jnp.float32) for rank in ranks
        ],
        compiler_params=pltpu.CompilerParams(vmem_limit_bytes=48 << 20),
    )(matrix, fields.reshape(count, size * levels, fields.shape[3]))


def decode_kernel(matrix_ref, f_ref, *refs, levels, ranks):
    code_refs, out_ref, scratch = refs[: len(ranks)], refs[-2], refs[-1]
    size = f_ref.shape[1] // levels
    scratch[...] = jnp.zeros_like(scratch)
    stacks = scratch.shape[0]

    def at_pair(pair, stack):
        for k in range(2):
            lanes = slice(128 * k, 128 * k + 128)
            start = size
            stack[:size, lanes] = f_ref[0, pl.ds(2 * pair + k, size, stride=levels), :]
            for rank, code_ref in zip(ranks, code_refs):
                stack[start : start + rank, lanes] = code_ref[
                    0, pl.ds(2 * pair + k, rank, stride=levels), :
                ]
                start += padded(rank)
        slope = jnp.dot(
            matrix_ref[...], split(stack[...]), preferred_element_type=jnp.float32
        )
        for k in range(2):
            out_ref[0, pl.ds(2 * pair + k, size, stride=levels), :] = slope[
                :, 128 * k : 128 * k + 128
            ]

    def some_pairs(group, carry):
        for k in range(stacks):
            at_pair(group * stacks + k, scratch.at[k])
        return carry

    lax.fori_loop(0, levels // (2 * stacks), some_pairs, 0)


def decoded(matrix, fields, codes, ranks, first, tiles):
    count, size, levels, _ = fields.shape
    width = 128
    cols = tiles * width
    total = size + sum(padded(rank) for rank in ranks)
    return pl.pallas_call(
        functools.partial(decode_kernel, levels=levels, ranks=ranks),
        grid=(count, cols // width),
        in_specs=[
            pl.BlockSpec(matrix.shape, lambda n, j: (0, 0)),
            pl.BlockSpec((1, size * levels, width), lambda n, j: (n, 0, first + j)),
        ]
        + [pl.BlockSpec((1, rank * levels, width), lambda n, j: (n, 0, j)) for rank in ranks],
        out_specs=pl.BlockSpec((1, size * levels, width), lambda n, j: (n, 0, j)),
        out_shape=jax.ShapeDtypeStruct((count, size * levels, cols), jnp.float32),
        scratch_shapes=[pltpu.VMEM((4, total, 2 * width), jnp.float32)],
        compiler_params=pltpu.CompilerParams(vmem_limit_bytes=48 << 20),
    )(matrix, fields.reshape(count, size * levels, fields.shape[3]), *codes).reshape(
        count, size, levels, cols
    )


def tendency_kernel(mask_ref, f_ref, beside_ref, halo_ref, s_ref, plane_ref, sx_ref, sy_ref, jb_ref, square_ref, *refs, leading):
    out_ref, hist_ref = refs[-2:]
    step = pl.program_id(0)
    rows, levels, cols = f_ref.shape[1:]

    @pl.when(step == 0)
    def _():
        hist_ref[...] = square_ref[...]

    level = lax.broadcasted_iota(jnp.int32, (levels, cols), 0)
    shape_factor = 1.0 - (level.astype(jnp.float32) + 0.5) / LEVELS
    first = level == 0
    last = level == levels - 1
    inverse = jnp.where(first | last, 1.0, 0.5)
    inner_side = lax.broadcasted_iota(jnp.int32, (levels, 128), 1) < 64
    if not leading:
        inner_side = ~inner_side
    row16 = lax.broadcasted_iota(jnp.int32, (16, cols), 0).astype(jnp.float32)
    targets = [(row16 + 16.0 * j).astype(jnp.bfloat16) for j in range(BINS // 16)]
    one = jnp.ones((16, cols), jnp.bfloat16)
    zero = jnp.zeros((16, cols), jnp.bfloat16)

    def row(x, carry):
        f = [f_ref[n, x] for n in range(4)]
        u, v, w, theta = f
        sx = jnp.broadcast_to(sx_ref[pl.ds(x, 1), :], (levels, cols))
        sy = jnp.broadcast_to(sy_ref[pl.ds(x, 1), :], (levels, cols))
        across = (w - shape_factor * (u * sx + v * sy)) * inverse
        v12 = v * (1.0 / 12.0)
        rate = FRINGE_RATE * mask_ref[step * rows + x].astype(jnp.float32)
        tend = []
        for n in range(4):
            g = f[n]
            above = jnp.where(last, g, pltpu.roll(g, levels - 1, 0))
            below = jnp.where(first, g, pltpu.roll(g, 1, 0))
            edge = jnp.where(inner_side, beside_ref[n, x], halo_ref[n, x])
            wide = jnp.concatenate([g, edge], axis=1)
            width = cols + 128
            d1 = (pltpu.roll(wide, width - 1, 1) - pltpu.roll(wide, 1, 1))[:, :cols]
            d2 = (pltpu.roll(wide, width - 2, 1) - pltpu.roll(wide, 2, 1))[:, :cols]
            t = (
                rate * (plane_ref[n] - g)
                - u * s_ref[n, x]
                - v12 * (8.0 * d1 - d2)
                - across * (above - below)
            )
            if n == 2:
                t = t + BUOYANCY * theta
            out_ref[n, x] = t
            tend.append(t)
        flux = (w + SECTION_DT * tend[2]) * (theta + SECTION_DT * tend[3])
        flux = flux.astype(jnp.bfloat16).astype(jnp.float32)
        bins = jb_ref[x]
        theta_bin = (bins >> (BINS.bit_length() - 1)).astype(jnp.float32)
        w_bin = (bins & (BINS - 1)).astype(jnp.float32)
        lhs, rhs = [], []
        for start in range(0, levels, 4):
            lq, rq = [], []
            for k in range(start, start + 4):
                tr = jnp.broadcast_to(theta_bin[k : k + 1], (16, cols)).astype(jnp.bfloat16)
                wr = jnp.broadcast_to(w_bin[k : k + 1], (16, cols)).astype(jnp.bfloat16)
                fr = jnp.broadcast_to(flux[k : k + 1], (16, cols)).astype(jnp.bfloat16)
                lq += [jnp.where(tr == i, one, zero) for i in targets]
                rq += [jnp.where(wr == i, fr, zero) for i in targets]
            lhs.append(jnp.concatenate(lq, 0))
            rhs.append(jnp.concatenate(rq, 0))
        hist_ref[...] += lax.dot_general(
            jnp.concatenate(lhs, 1),
            jnp.concatenate(rhs, 1),
            (((1,), (1,)), ((), ())),
            preferred_element_type=jnp.float32,
        )
        return carry

    lax.fori_loop(0, rows, row, 0, unroll=8)


def tendency_half(mask, fields, halo, stream_slope, plane, slope_x, slope_y, jbin, square, previous):
    count, size, levels, total = fields.shape
    cols, rows = total // 2, 8
    leading = previous is None
    c = 0 if leading else 1
    tile = cols // 128 if leading else cols // 128 - 1
    big = pl.BlockSpec((count, rows, levels, cols), lambda i, m: (0, i, 0, c))
    plain = pl.BlockSpec((rows, cols), lambda i, m: (i, c))
    whole = pl.BlockSpec(square.shape, lambda i, m: (0, 0))
    return pl.pallas_call(
        functools.partial(tendency_kernel, leading=leading),
        grid_spec=pltpu.PrefetchScalarGridSpec(
            num_scalar_prefetch=1,
            grid=(size // rows,),
            in_specs=[
                big,
                pl.BlockSpec((count, rows, levels, 128), lambda i, m: (0, i, 0, tile)),
                pl.BlockSpec((count, rows, levels, 128), lambda i, m: (0, i, 0, 0)),
                pl.BlockSpec((count, rows, levels, cols), lambda i, m: (0, i, 0, 0)),
                pl.BlockSpec((count, levels, cols), lambda i, m: (0, 0, 0)),
                plain,
                plain,
                pl.BlockSpec((rows, levels, cols), lambda i, m: (i, 0, c)),
                whole,
            ]
            + ([] if leading else [pl.BlockSpec(memory_space=pl.ANY)]),
            out_specs=[big, whole],
        ),
        out_shape=[
            jax.ShapeDtypeStruct(fields.shape, jnp.float32),
            jax.ShapeDtypeStruct(square.shape, jnp.float32),
        ],
        input_output_aliases={} if leading else {10: 0},
        compiler_params=pltpu.CompilerParams(vmem_limit_bytes=48 << 20),
    )(mask, fields, fields, halo, stream_slope, plane, slope_x, slope_y, jbin, square,
      *([] if leading else [previous]))


def shards(fields, slope_x, slope_y, fringe_mask, plane_x, joint_bin):
    field_count, local_rows, levels, local_cols = fields.shape
    span, stream = lax.axis_size("gy"), lax.axis_size("gx")
    total_x, total_y = local_rows * stream, local_cols * span
    encoder, decoder, ranks = operators(total_x, local_rows)
    half = local_cols // 256

    def moved(code, distance):
        return lax.ppermute(code, "gx", [(i, (i + distance) % stream) for i in range(stream)])

    owner = plane_x[0] // local_rows
    own_row = lax.dynamic_index_in_dim(fields, plane_x[0] % local_rows, 1, keepdims=False)
    own_row = jnp.where(lax.axis_index("gx") == owner, own_row, jnp.zeros_like(own_row))
    picked = (lax.iota(jnp.int32, local_rows) == plane_x[0] % local_rows) & (
        lax.axis_index("gx") == owner
    )
    picked = picked.astype(jnp.bfloat16)
    nothing = jnp.zeros_like(picked)
    picked = jnp.concatenate([picked, nothing, nothing, picked, nothing, picked])
    last_rows = np.cumsum([0, *map(padded, ranks)])[:-1] + np.array(ranks) - 1
    plane_rows = np.isin(np.arange(encoder.shape[0]), last_rows)[:, None]
    encoder = jnp.where(plane_rows, picked[None, :], encoder)
    distances = range(1, stream)
    codes = encoded(encoder, fields, ranks, 0, half)
    codes = [moved(code, d) for code, d in zip(codes, distances)]
    later = encoded(encoder, fields, ranks, half, half)
    forward = [(i, (i + 1) % span) for i in range(span)]
    backward = [(target, source) for source, target in forward]
    low = lax.ppermute(fields[..., -2:], "gy", forward)
    high = lax.ppermute(fields[..., :2], "gy", backward)
    halo = jnp.concatenate([high, jnp.zeros(fields.shape[:3] + (124,), jnp.float32), low], -1)
    codes, later, halo = lax.optimization_barrier((codes, later, halo))
    held = [d for d in distances if 2 < d < stream - 2 and 2 * d != stream]
    later = [code if d in held else moved(code, d) for code, d in zip(later, distances)]
    stream_slope = decoded(decoder, fields, codes, ranks, 0, half)
    stream_slope, *rest = lax.optimization_barrier((stream_slope, *[later[d - 1] for d in held]))
    for code, d in zip(rest, held):
        later[d - 1] = moved(code, d)
    tendency = None
    square = jnp.zeros((4 * BINS, 4 * BINS), jnp.float32)
    for part in range(2):
        if part:
            later, tendency = lax.optimization_barrier((later, tendency))
            stream_slope = decoded(decoder, fields, later, ranks, half, half)
        arrived = later if part else codes
        plane = own_row[..., 128 * half * part : 128 * half * (part + 1)]
        for code, rank in zip(arrived, ranks):
            plane = plane + code[:, (rank - 1) * levels :]
        tendency, square = tendency_half(
            fringe_mask, fields, halo, stream_slope, plane, slope_x, slope_y, joint_bin, square, tendency
        )
    sums = sum(square[BINS * i : BINS * i + BINS, BINS * i : BINS * i + BINS] for i in range(4))
    scale = (BINS * BINS / (total_x * total_y * levels)) ** 0.5
    row_share, col_share = BINS // stream, BINS // span
    pieces_of = sums.reshape(stream, row_share, span, col_share).transpose(0, 2, 1, 3)
    pieces_of = pieces_of.reshape(stream * span, row_share * col_share)
    received = lax.all_to_all(pieces_of, ("gx", "gy"), split_axis=0, concat_axis=0, tiled=True)
    own_sums = received.sum(0).reshape(row_share, col_share)
    return tendency, own_sums * scale


def solution(mesh):
    placed = (
        P(None, "gx", None, "gy"),
        P("gx", "gy"),
        P("gx", "gy"),
        P("gx"),
        P(),
        P("gx", None, "gy"),
    )
    return jax.shard_map(
        shards,
        mesh=mesh,
        in_specs=placed,
        out_specs=(P(None, "gx", None, "gy"), P("gx", "gy")),
        check_vma=False,
    )
```

```python
import functools
import math

import jax
import jax.numpy as jnp
import ml_dtypes
import numpy as np
from jax import lax
from jax.experimental import pallas as pl
from jax.experimental.pallas import tpu as pltpu
from jax.sharding import PartitionSpec as P

LEVELS = 384
BINS = 64


FRINGE_RATE = 0.5
BUOYANCY = 0.5
SECTION_DT = 0.25

FACTOR_TOLERANCE = 1e-9


def padded(rank):
    return -(-rank // 8) * 8


def derivative_block(count, size, distance):
    table = np.zeros(count)
    for k in range(1, count):
        value = math.pi / count * math.cos(math.pi * k / count) / math.sin(math.pi * k / count)
        table[k] = round(value * 2.0**45) / 2.0**45 * (1 if k % 2 == 0 else -1)
    offset = np.arange(size)[:, None] - np.arange(size)[None, :] + distance * size
    return table[offset % count]


def factored(block, tolerance):
    rest = block.copy()
    left, right = [], []
    while True:
        row, col = np.unravel_index(np.argmax(np.abs(rest)), rest.shape)
        pivot = rest[row, col]
        if abs(pivot) <= tolerance and left:
            break
        left.append(rest[:, col] / pivot)
        right.append(rest[row, :].copy())
        rest = rest - left[-1][:, None] * right[-1][None, :]
    return np.stack(left, 1), np.stack(right, 0)


def pieces(matrix):
    rest, parts = matrix, []
    for _ in range(3):
        parts.append(rest.astype(ml_dtypes.bfloat16))
        rest = rest - parts[-1].astype(np.float64)
    high, middle, low = parts
    return np.concatenate([high, middle, low, high, middle, high], 1)


def operators(count, size):
    ranks, encode, decode = [], [], [derivative_block(count, size, 0)]
    for distance in range(1, count // size):
        left, right = factored(derivative_block(count, size, distance), FACTOR_TOLERANCE)
        ranks.append(left.shape[1] + 1)
        spare = padded(ranks[-1]) - left.shape[1]
        decode.append(np.pad(left, ((0, 0), (0, spare))))
        encode.append(np.pad(right, ((0, spare), (0, 0))))
    return pieces(np.concatenate(encode, 0)), pieces(np.concatenate(decode, 1)), tuple(ranks)


def split(value):
    high = value.astype(jnp.bfloat16)
    rest = value - high.astype(jnp.float32)
    middle = rest.astype(jnp.bfloat16)
    low = (rest - middle.astype(jnp.float32)).astype(jnp.bfloat16)
    return jnp.concatenate([high, high, high, middle, middle, low], 0)


def encode_kernel(matrix_ref, f_ref, *out_refs, levels, ranks):
    size = f_ref.shape[1] // levels

    def at_pair(pair, carry):
        parts = [
            f_ref[0, pl.ds(2 * pair + k, size, stride=levels), :] for k in range(2)
        ]
        coded = jnp.dot(
            matrix_ref[...],
            split(jnp.concatenate(parts, 1)),
            preferred_element_type=jnp.float32,
        )
        start = 0
        for rank, out_ref in zip(ranks, out_refs):
            for k in range(2):
                out_ref[0, pl.ds(2 * pair + k, rank, stride=levels), :] = coded[
                    start : start + rank, 128 * k : 128 * k + 128
                ]
            start += padded(rank)
        return carry

    lax.fori_loop(0, levels // 2, at_pair, 0, unroll=4)


def encoded(matrix, fields, ranks, first, tiles):
    count, size, levels, _ = fields.shape
    width = 128
    cols = tiles * width
    return pl.pallas_call(
        functools.partial(encode_kernel, levels=levels, ranks=ranks),
        grid=(count, cols // width),
        in_specs=[
            pl.BlockSpec(matrix.shape, lambda n, j: (0, 0)),
            pl.BlockSpec((1, size * levels, width), lambda n, j: (n, 0, first + j)),
        ],
        out_specs=[
            pl.BlockSpec((1, rank * levels, width), lambda n, j: (n, 0, j)) for rank in ranks
        ],
        out_shape=[
            jax.ShapeDtypeStruct((count, rank * levels, cols), jnp.float32) for rank in ranks
        ],
        compiler_params=pltpu.CompilerParams(vmem_limit_bytes=48 << 20),
    )(matrix, fields.reshape(count, size * levels, fields.shape[3]))


def decode_kernel(matrix_ref, f_ref, *refs, levels, ranks):
    code_refs, out_ref, scratch = refs[: len(ranks)], refs[-2], refs[-1]
    size = f_ref.shape[1] // levels
    scratch[...] = jnp.zeros_like(scratch)
    stacks = scratch.shape[0]

    def at_pair(pair, stack):
        for k in range(2):
            lanes = slice(128 * k, 128 * k + 128)
            start = size
            stack[:size, lanes] = f_ref[0, pl.ds(2 * pair + k, size, stride=levels), :]
            for rank, code_ref in zip(ranks, code_refs):
                stack[start : start + rank, lanes] = code_ref[
                    0, pl.ds(2 * pair + k, rank, stride=levels), :
                ]
                start += padded(rank)
        slope = jnp.dot(
            matrix_ref[...], split(stack[...]), preferred_element_type=jnp.float32
        )
        for k in range(2):
            out_ref[0, pl.ds(2 * pair + k, size, stride=levels), :] = slope[
                :, 128 * k : 128 * k + 128
            ]

    def some_pairs(group, carry):
        for k in range(stacks):
            at_pair(group * stacks + k, scratch.at[k])
        return carry

    lax.fori_loop(0, levels // (2 * stacks), some_pairs, 0)


def decoded(matrix, fields, codes, ranks, first, tiles):
    count, size, levels, _ = fields.shape
    width = 128
    cols = tiles * width
    total = size + sum(padded(rank) for rank in ranks)
    return pl.pallas_call(
        functools.partial(decode_kernel, levels=levels, ranks=ranks),
        grid=(count, cols // width),
        in_specs=[
            pl.BlockSpec(matrix.shape, lambda n, j: (0, 0)),
            pl.BlockSpec((1, size * levels, width), lambda n, j: (n, 0, first + j)),
        ]
        + [pl.BlockSpec((1, rank * levels, width), lambda n, j: (n, 0, j)) for rank in ranks],
        out_specs=pl.BlockSpec((1, size * levels, width), lambda n, j: (n, 0, j)),
        out_shape=jax.ShapeDtypeStruct((count, size * levels, cols), jnp.float32),
        scratch_shapes=[pltpu.VMEM((4, total, 2 * width), jnp.float32)],
        compiler_params=pltpu.CompilerParams(vmem_limit_bytes=48 << 20),
    )(matrix, fields.reshape(count, size * levels, fields.shape[3]), *codes).reshape(
        count, size, levels, cols
    )


def tendency_kernel(mask_ref, f_ref, beside_ref, halo_ref, s_ref, plane_ref, sx_ref, sy_ref, jb_ref, square_ref, *refs, leading):
    out_ref, hist_ref = refs[-2:]
    step = pl.program_id(0)
    rows, levels, cols = f_ref.shape[1:]

    @pl.when(step == 0)
    def _():
        hist_ref[...] = square_ref[...]

    level = lax.broadcasted_iota(jnp.int32, (levels, cols), 0)
    shape_factor = 1.0 - (level.astype(jnp.float32) + 0.5) / LEVELS
    first = level == 0
    last = level == levels - 1
    inverse = jnp.where(first | last, 1.0, 0.5)
    inner_side = lax.broadcasted_iota(jnp.int32, (levels, 128), 1) < 64
    if not leading:
        inner_side = ~inner_side
    row16 = lax.broadcasted_iota(jnp.int32, (16, cols), 0).astype(jnp.float32)
    targets = [(row16 + 16.0 * j).astype(jnp.bfloat16) for j in range(BINS // 16)]
    one = jnp.ones((16, cols), jnp.bfloat16)
    zero = jnp.zeros((16, cols), jnp.bfloat16)

    def row(x, carry):
        f = [f_ref[n, x] for n in range(4)]
        u, v, w, theta = f
        sx = jnp.broadcast_to(sx_ref[pl.ds(x, 1), :], (levels, cols))
        sy = jnp.broadcast_to(sy_ref[pl.ds(x, 1), :], (levels, cols))
        across = (w - shape_factor * (u * sx + v * sy)) * inverse
        v12 = v * (1.0 / 12.0)
        rate = FRINGE_RATE * mask_ref[step * rows + x].astype(jnp.float32)
        tend = []
        for n in range(4):
            g = f[n]
            above = jnp.where(last, g, pltpu.roll(g, levels - 1, 0))
            below = jnp.where(first, g, pltpu.roll(g, 1, 0))
            edge = jnp.where(inner_side, beside_ref[n, x], halo_ref[n, x])
            wide = jnp.concatenate([g, edge], axis=1)
            width = cols + 128
            d1 = (pltpu.roll(wide, width - 1, 1) - pltpu.roll(wide, 1, 1))[:, :cols]
            d2 = (pltpu.roll(wide, width - 2, 1) - pltpu.roll(wide, 2, 1))[:, :cols]
            t = (
                rate * (plane_ref[n] - g)
                - u * s_ref[n, x]
                - v12 * (8.0 * d1 - d2)
                - across * (above - below)
            )
            if n == 2:
                t = t + BUOYANCY * theta
            out_ref[n, x] = t
            tend.append(t)
        flux = (w + SECTION_DT * tend[2]) * (theta + SECTION_DT * tend[3])
        flux = flux.astype(jnp.bfloat16).astype(jnp.float32)
        bins = jb_ref[x]
        theta_bin = (bins >> (BINS.bit_length() - 1)).astype(jnp.float32)
        w_bin = (bins & (BINS - 1)).astype(jnp.float32)
        lhs, rhs = [], []
        for start in range(0, levels, 4):
            lq, rq = [], []
            for k in range(start, start + 4):
                tr = jnp.broadcast_to(theta_bin[k : k + 1], (16, cols)).astype(jnp.bfloat16)
                wr = jnp.broadcast_to(w_bin[k : k + 1], (16, cols)).astype(jnp.bfloat16)
                fr = jnp.broadcast_to(flux[k : k + 1], (16, cols)).astype(jnp.bfloat16)
                lq += [jnp.where(tr == i, one, zero) for i in targets]
                rq += [jnp.where(wr == i, fr, zero) for i in targets]
            lhs.append(jnp.concatenate(lq, 0))
            rhs.append(jnp.concatenate(rq, 0))
        hist_ref[...] += lax.dot_general(
            jnp.concatenate(lhs, 1),
            jnp.concatenate(rhs, 1),
            (((1,), (1,)), ((), ())),
            preferred_element_type=jnp.float32,
        )
        return carry

    lax.fori_loop(0, rows, row, 0, unroll=8)


def tendency_half(mask, fields, halo, stream_slope, plane, slope_x, slope_y, jbin, square, previous):
    count, size, levels, total = fields.shape
    cols, rows = total // 2, 8
    leading = previous is None
    c = 0 if leading else 1
    tile = cols // 128 if leading else cols // 128 - 1
    big = pl.BlockSpec((count, rows, levels, cols), lambda i, m: (0, i, 0, c))
    plain = pl.BlockSpec((rows, cols), lambda i, m: (i, c))
    whole = pl.BlockSpec(square.shape, lambda i, m: (0, 0))
    return pl.pallas_call(
        functools.partial(tendency_kernel, leading=leading),
        grid_spec=pltpu.PrefetchScalarGridSpec(
            num_scalar_prefetch=1,
            grid=(size // rows,),
            in_specs=[
                big,
                pl.BlockSpec((count, rows, levels, 128), lambda i, m: (0, i, 0, tile)),
                pl.BlockSpec((count, rows, levels, 128), lambda i, m: (0, i, 0, 0)),
                pl.BlockSpec((count, rows, levels, cols), lambda i, m: (0, i, 0, 0)),
                pl.BlockSpec((count, levels, cols), lambda i, m: (0, 0, 0)),
                plain,
                plain,
                pl.BlockSpec((rows, levels, cols), lambda i, m: (i, 0, c)),
                whole,
            ]
            + ([] if leading else [pl.BlockSpec(memory_space=pl.ANY)]),
            out_specs=[big, whole],
        ),
        out_shape=[
            jax.ShapeDtypeStruct(fields.shape, jnp.float32),
            jax.ShapeDtypeStruct(square.shape, jnp.float32),
        ],
        input_output_aliases={} if leading else {10: 0},
        compiler_params=pltpu.CompilerParams(vmem_limit_bytes=48 << 20),
    )(mask, fields, fields, halo, stream_slope, plane, slope_x, slope_y, jbin, square,
      *([] if leading else [previous]))


def shards(fields, slope_x, slope_y, fringe_mask, plane_x, joint_bin):
    field_count, local_rows, levels, local_cols = fields.shape
    span, stream = lax.axis_size("gy"), lax.axis_size("gx")
    total_x, total_y = local_rows * stream, local_cols * span
    encoder, decoder, ranks = operators(total_x, local_rows)
    half = local_cols // 256

    def moved(code, distance):
        return lax.ppermute(code, "gx", [(i, (i + distance) % stream) for i in range(stream)])

    owner = plane_x[0] // local_rows
    own_row = lax.dynamic_index_in_dim(fields, plane_x[0] % local_rows, 1, keepdims=False)
    own_row = jnp.where(lax.axis_index("gx") == owner, own_row, jnp.zeros_like(own_row))
    picked = (lax.iota(jnp.int32, local_rows) == plane_x[0] % local_rows) & (
        lax.axis_index("gx") == owner
    )
    picked = picked.astype(jnp.bfloat16)
    nothing = jnp.zeros_like(picked)
    picked = jnp.concatenate([picked, nothing, nothing, picked, nothing, picked])
    last_rows = np.cumsum([0, *map(padded, ranks)])[:-1] + np.array(ranks) - 1
    plane_rows = np.isin(np.arange(encoder.shape[0]), last_rows)[:, None]
    encoder = jnp.where(plane_rows, picked[None, :], encoder)
    distances = range(1, stream)
    codes = encoded(encoder, fields, ranks, 0, half)
    codes = [moved(code, d) for code, d in zip(codes, distances)]
    later = encoded(encoder, fields, ranks, half, half)
    forward = [(i, (i + 1) % span) for i in range(span)]
    backward = [(target, source) for source, target in forward]
    low = lax.ppermute(fields[..., -2:], "gy", forward)
    high = lax.ppermute(fields[..., :2], "gy", backward)
    halo = jnp.concatenate([high, jnp.zeros(fields.shape[:3] + (124,), jnp.float32), low], -1)
    codes, later, halo = lax.optimization_barrier((codes, later, halo))
    held = [d for d in distances if 2 < d < stream - 2 and 2 * d != stream]
    later = [code if d in held else moved(code, d) for code, d in zip(later, distances)]
    stream_slope = decoded(decoder, fields, codes, ranks, 0, half)
    tendency = None
    square = jnp.zeros((4 * BINS, 4 * BINS), jnp.float32)
    for part in range(2):
        if part:
            later, tendency = lax.optimization_barrier((later, tendency))
            later = [moved(code, d) if d in held else code for code, d in zip(later, distances)]
            stream_slope = decoded(decoder, fields, later, ranks, half, half)
        arrived = later if part else codes
        plane = own_row[..., 128 * half * part : 128 * half * (part + 1)]
        for code, rank in zip(arrived, ranks):
            plane = plane + code[:, (rank - 1) * levels :]
        tendency, square = tendency_half(
            fringe_mask, fields, halo, stream_slope, plane, slope_x, slope_y, joint_bin, square, tendency
        )
    sums = sum(square[BINS * i : BINS * i + BINS, BINS * i : BINS * i + BINS] for i in range(4))
    scale = (BINS * BINS / (total_x * total_y * levels)) ** 0.5
    row_share, col_share = BINS // stream, BINS // span
    pieces_of = sums.reshape(stream, row_share, span, col_share).transpose(0, 2, 1, 3)
    pieces_of = pieces_of.reshape(stream * span, row_share * col_share)
    received = lax.all_to_all(pieces_of, ("gx", "gy"), split_axis=0, concat_axis=0, tiled=True)
    own_sums = received.sum(0).reshape(row_share, col_share)
    return tendency, own_sums * scale


def solution(mesh):
    placed = (
        P(None, "gx", None, "gy"),
        P("gx", "gy"),
        P("gx", "gy"),
        P("gx"),
        P(),
        P("gx", None, "gy"),
    )
    return jax.shard_map(
        shards,
        mesh=mesh,
        in_specs=placed,
        out_specs=(P(None, "gx", None, "gy"), P("gx", "gy")),
        check_vma=False,
    )
```

```python
import functools
import math

import jax
import jax.numpy as jnp
import ml_dtypes
import numpy as np
from jax import lax
from jax.experimental import pallas as pl
from jax.experimental.pallas import tpu as pltpu
from jax.sharding import PartitionSpec as P

LEVELS = 384
BINS = 64


FRINGE_RATE = 0.5
BUOYANCY = 0.5
SECTION_DT = 0.25

FACTOR_TOLERANCE = 1e-9


def padded(rank):
    return -(-rank // 8) * 8


def derivative_block(count, size, distance):
    table = np.zeros(count)
    for k in range(1, count):
        value = math.pi / count * math.cos(math.pi * k / count) / math.sin(math.pi * k / count)
        table[k] = round(value * 2.0**45) / 2.0**45 * (1 if k % 2 == 0 else -1)
    offset = np.arange(size)[:, None] - np.arange(size)[None, :] + distance * size
    return table[offset % count]


def factored(block, tolerance):
    rest = block.copy()
    left, right = [], []
    while True:
        row, col = np.unravel_index(np.argmax(np.abs(rest)), rest.shape)
        pivot = rest[row, col]
        if abs(pivot) <= tolerance and left:
            break
        left.append(rest[:, col] / pivot)
        right.append(rest[row, :].copy())
        rest = rest - left[-1][:, None] * right[-1][None, :]
    return np.stack(left, 1), np.stack(right, 0)


def pieces(matrix):
    rest, parts = matrix, []
    for _ in range(3):
        parts.append(rest.astype(ml_dtypes.bfloat16))
        rest = rest - parts[-1].astype(np.float64)
    high, middle, low = parts
    return np.concatenate([high, middle, low, high, middle, high], 1)


def operators(count, size):
    ranks, encode, decode = [], [], [derivative_block(count, size, 0)]
    for distance in range(1, count // size):
        left, right = factored(derivative_block(count, size, distance), FACTOR_TOLERANCE)
        ranks.append(left.shape[1] + 1)
        spare = padded(ranks[-1]) - left.shape[1]
        decode.append(np.pad(left, ((0, 0), (0, spare))))
        encode.append(np.pad(right, ((0, spare), (0, 0))))
    return pieces(np.concatenate(encode, 0)), pieces(np.concatenate(decode, 1)), tuple(ranks)


def split(value):
    high = value.astype(jnp.bfloat16)
    rest = value - high.astype(jnp.float32)
    middle = rest.astype(jnp.bfloat16)
    low = (rest - middle.astype(jnp.float32)).astype(jnp.bfloat16)
    return jnp.concatenate([high, high, high, middle, middle, low], 0)


def encode_kernel(matrix_ref, f_ref, *out_refs, levels, ranks):
    size = f_ref.shape[1] // levels

    def at_pair(pair, carry):
        parts = [
            f_ref[0, pl.ds(2 * pair + k, size, stride=levels), :] for k in range(2)
        ]
        coded = jnp.dot(
            matrix_ref[...],
            split(jnp.concatenate(parts, 1)),
            preferred_element_type=jnp.float32,
        )
        start = 0
        for rank, out_ref in zip(ranks, out_refs):
            for k in range(2):
                out_ref[0, pl.ds(2 * pair + k, rank, stride=levels), :] = coded[
                    start : start + rank, 128 * k : 128 * k + 128
                ]
            start += padded(rank)
        return carry

    lax.fori_loop(0, levels // 2, at_pair, 0, unroll=4)


def encoded(matrix, fields, ranks, first, tiles):
    count, size, levels, _ = fields.shape
    width = 128
    cols = tiles * width
    return pl.pallas_call(
        functools.partial(encode_kernel, levels=levels, ranks=ranks),
        grid=(count, cols // width),
        in_specs=[
            pl.BlockSpec(matrix.shape, lambda n, j: (0, 0)),
            pl.BlockSpec((1, size * levels, width), lambda n, j: (n, 0, first + j)),
        ],
        out_specs=[
            pl.BlockSpec((1, rank * levels, width), lambda n, j: (n, 0, j)) for rank in ranks
        ],
        out_shape=[
            jax.ShapeDtypeStruct((count, rank * levels, cols), jnp.float32) for rank in ranks
        ],
        compiler_params=pltpu.CompilerParams(vmem_limit_bytes=48 << 20),
    )(matrix, fields.reshape(count, size * levels, fields.shape[3]))


def decode_kernel(matrix_ref, f_ref, *refs, levels, ranks):
    code_refs, out_ref, scratch = refs[: len(ranks)], refs[-2], refs[-1]
    size = f_ref.shape[1] // levels
    scratch[...] = jnp.zeros_like(scratch)
    stacks = scratch.shape[0]

    def at_pair(pair, stack):
        for k in range(2):
            lanes = slice(128 * k, 128 * k + 128)
            start = size
            stack[:size, lanes] = f_ref[0, pl.ds(2 * pair + k, size, stride=levels), :]
            for rank, code_ref in zip(ranks, code_refs):
                stack[start : start + rank, lanes] = code_ref[
                    0, pl.ds(2 * pair + k, rank, stride=levels), :
                ]
                start += padded(rank)
        slope = jnp.dot(
            matrix_ref[...], split(stack[...]), preferred_element_type=jnp.float32
        )
        for k in range(2):
            out_ref[0, pl.ds(2 * pair + k, size, stride=levels), :] = slope[
                :, 128 * k : 128 * k + 128
            ]

    def some_pairs(group, carry):
        for k in range(stacks):
            at_pair(group * stacks + k, scratch.at[k])
        return carry

    lax.fori_loop(0, levels // (2 * stacks), some_pairs, 0)


def decoded(matrix, fields, codes, ranks, first, tiles):
    count, size, levels, _ = fields.shape
    width = 128
    cols = tiles * width
    total = size + sum(padded(rank) for rank in ranks)
    return pl.pallas_call(
        functools.partial(decode_kernel, levels=levels, ranks=ranks),
        grid=(count, cols // width),
        in_specs=[
            pl.BlockSpec(matrix.shape, lambda n, j: (0, 0)),
            pl.BlockSpec((1, size * levels, width), lambda n, j: (n, 0, first + j)),
        ]
        + [pl.BlockSpec((1, rank * levels, width), lambda n, j: (n, 0, j)) for rank in ranks],
        out_specs=pl.BlockSpec((1, size * levels, width), lambda n, j: (n, 0, j)),
        out_shape=jax.ShapeDtypeStruct((count, size * levels, cols), jnp.float32),
        scratch_shapes=[pltpu.VMEM((8, total, 2 * width), jnp.float32)],
        compiler_params=pltpu.CompilerParams(vmem_limit_bytes=48 << 20),
    )(matrix, fields.reshape(count, size * levels, fields.shape[3]), *codes).reshape(
        count, size, levels, cols
    )


def tendency_kernel(mask_ref, f_ref, beside_ref, halo_ref, s_ref, plane_ref, sx_ref, sy_ref, jb_ref, square_ref, *refs, leading):
    out_ref, hist_ref = refs[-2:]
    step = pl.program_id(0)
    rows, levels, cols = f_ref.shape[1:]

    @pl.when(step == 0)
    def _():
        hist_ref[...] = square_ref[...]

    level = lax.broadcasted_iota(jnp.int32, (levels, cols), 0)
    shape_factor = 1.0 - (level.astype(jnp.float32) + 0.5) / LEVELS
    first = level == 0
    last = level == levels - 1
    inverse = jnp.where(first | last, 1.0, 0.5)
    inner_side = lax.broadcasted_iota(jnp.int32, (levels, 128), 1) < 64
    if not leading:
        inner_side = ~inner_side
    row16 = lax.broadcasted_iota(jnp.int32, (16, cols), 0).astype(jnp.float32)
    targets = [(row16 + 16.0 * j).astype(jnp.bfloat16) for j in range(BINS // 16)]
    one = jnp.ones((16, cols), jnp.bfloat16)
    zero = jnp.zeros((16, cols), jnp.bfloat16)

    def row(x, carry):
        f = [f_ref[n, x] for n in range(4)]
        u, v, w, theta = f
        sx = jnp.broadcast_to(sx_ref[pl.ds(x, 1), :], (levels, cols))
        sy = jnp.broadcast_to(sy_ref[pl.ds(x, 1), :], (levels, cols))
        across = (w - shape_factor * (u * sx + v * sy)) * inverse
        v12 = v * (1.0 / 12.0)
        rate = FRINGE_RATE * mask_ref[step * rows + x].astype(jnp.float32)
        tend = []
        for n in range(4):
            g = f[n]
            above = jnp.where(last, g, pltpu.roll(g, levels - 1, 0))
            below = jnp.where(first, g, pltpu.roll(g, 1, 0))
            edge = jnp.where(inner_side, beside_ref[n, x], halo_ref[n, x])
            wide = jnp.concatenate([g, edge], axis=1)
            width = cols + 128
            d1 = (pltpu.roll(wide, width - 1, 1) - pltpu.roll(wide, 1, 1))[:, :cols]
            d2 = (pltpu.roll(wide, width - 2, 1) - pltpu.roll(wide, 2, 1))[:, :cols]
            t = (
                rate * (plane_ref[n] - g)
                - u * s_ref[n, x]
                - v12 * (8.0 * d1 - d2)
                - across * (above - below)
            )
            if n == 2:
                t = t + BUOYANCY * theta
            out_ref[n, x] = t
            tend.append(t)
        flux = (w + SECTION_DT * tend[2]) * (theta + SECTION_DT * tend[3])
        flux = flux.astype(jnp.bfloat16).astype(jnp.float32)
        bins = jb_ref[x]
        theta_bin = (bins >> (BINS.bit_length() - 1)).astype(jnp.float32)
        w_bin = (bins & (BINS - 1)).astype(jnp.float32)
        lhs, rhs = [], []
        for start in range(0, levels, 4):
            lq, rq = [], []
            for k in range(start, start + 4):
                tr = jnp.broadcast_to(theta_bin[k : k + 1], (16, cols)).astype(jnp.bfloat16)
                wr = jnp.broadcast_to(w_bin[k : k + 1], (16, cols)).astype(jnp.bfloat16)
                fr = jnp.broadcast_to(flux[k : k + 1], (16, cols)).astype(jnp.bfloat16)
                lq += [jnp.where(tr == i, one, zero) for i in targets]
                rq += [jnp.where(wr == i, fr, zero) for i in targets]
            lhs.append(jnp.concatenate(lq, 0))
            rhs.append(jnp.concatenate(rq, 0))
        hist_ref[...] += lax.dot_general(
            jnp.concatenate(lhs, 1),
            jnp.concatenate(rhs, 1),
            (((1,), (1,)), ((), ())),
            preferred_element_type=jnp.float32,
        )
        return carry

    lax.fori_loop(0, rows, row, 0, unroll=16)


def tendency_half(mask, fields, halo, stream_slope, plane, slope_x, slope_y, jbin, square, previous):
    count, size, levels, total = fields.shape
    cols, rows = total // 2, 16
    leading = previous is None
    c = 0 if leading else 1
    tile = cols // 128 if leading else cols // 128 - 1
    big = pl.BlockSpec((count, rows, levels, cols), lambda i, m: (0, i, 0, c))
    plain = pl.BlockSpec((rows, cols), lambda i, m: (i, c))
    whole = pl.BlockSpec(square.shape, lambda i, m: (0, 0))
    return pl.pallas_call(
        functools.partial(tendency_kernel, leading=leading),
        grid_spec=pltpu.PrefetchScalarGridSpec(
            num_scalar_prefetch=1,
            grid=(size // rows,),
            in_specs=[
                big,
                pl.BlockSpec((count, rows, levels, 128), lambda i, m: (0, i, 0, tile)),
                pl.BlockSpec((count, rows, levels, 128), lambda i, m: (0, i, 0, 0)),
                pl.BlockSpec((count, rows, levels, cols), lambda i, m: (0, i, 0, 0)),
                pl.BlockSpec((count, levels, cols), lambda i, m: (0, 0, 0)),
                plain,
                plain,
                pl.BlockSpec((rows, levels, cols), lambda i, m: (i, 0, c)),
                whole,
            ]
            + ([] if leading else [pl.BlockSpec(memory_space=pl.ANY)]),
            out_specs=[big, whole],
        ),
        out_shape=[
            jax.ShapeDtypeStruct(fields.shape, jnp.float32),
            jax.ShapeDtypeStruct(square.shape, jnp.float32),
        ],
        input_output_aliases={} if leading else {10: 0},
        compiler_params=pltpu.CompilerParams(vmem_limit_bytes=48 << 20),
    )(mask, fields, fields, halo, stream_slope, plane, slope_x, slope_y, jbin, square,
      *([] if leading else [previous]))


def shards(fields, slope_x, slope_y, fringe_mask, plane_x, joint_bin):
    field_count, local_rows, levels, local_cols = fields.shape
    span, stream = lax.axis_size("gy"), lax.axis_size("gx")
    total_x, total_y = local_rows * stream, local_cols * span
    encoder, decoder, ranks = operators(total_x, local_rows)
    half = local_cols // 256

    def moved(code, distance):
        return lax.ppermute(code, "gx", [(i, (i + distance) % stream) for i in range(stream)])

    owner = plane_x[0] // local_rows
    own_row = lax.dynamic_index_in_dim(fields, plane_x[0] % local_rows, 1, keepdims=False)
    own_row = jnp.where(lax.axis_index("gx") == owner, own_row, jnp.zeros_like(own_row))
    picked = (lax.iota(jnp.int32, local_rows) == plane_x[0] % local_rows) & (
        lax.axis_index("gx") == owner
    )
    picked = picked.astype(jnp.bfloat16)
    nothing = jnp.zeros_like(picked)
    picked = jnp.concatenate([picked, nothing, nothing, picked, nothing, picked])
    last_rows = np.cumsum([0, *map(padded, ranks)])[:-1] + np.array(ranks) - 1
    plane_rows = np.isin(np.arange(encoder.shape[0]), last_rows)[:, None]
    encoder = jnp.where(plane_rows, picked[None, :], encoder)
    distances = range(1, stream)
    codes = encoded(encoder, fields, ranks, 0, half)
    codes = [moved(code, d) for code, d in zip(codes, distances)]
    later = encoded(encoder, fields, ranks, half, half)
    forward = [(i, (i + 1) % span) for i in range(span)]
    backward = [(target, source) for source, target in forward]
    low = lax.ppermute(fields[..., -2:], "gy", forward)
    high = lax.ppermute(fields[..., :2], "gy", backward)
    halo = jnp.concatenate([high, jnp.zeros(fields.shape[:3] + (124,), jnp.float32), low], -1)
    codes, later, halo = lax.optimization_barrier((codes, later, halo))
    held = [d for d in distances if 2 < d < stream - 2 and 2 * d != stream]
    later = [code if d in held else moved(code, d) for code, d in zip(later, distances)]
    stream_slope = decoded(decoder, fields, codes, ranks, 0, half)
    tendency = None
    square = jnp.zeros((4 * BINS, 4 * BINS), jnp.float32)
    for part in range(2):
        if part:
            later, tendency = lax.optimization_barrier((later, tendency))
            later = [moved(code, d) if d in held else code for code, d in zip(later, distances)]
            stream_slope = decoded(decoder, fields, later, ranks, half, half)
        arrived = later if part else codes
        plane = own_row[..., 128 * half * part : 128 * half * (part + 1)]
        for code, rank in zip(arrived, ranks):
            plane = plane + code[:, (rank - 1) * levels :]
        tendency, square = tendency_half(
            fringe_mask, fields, halo, stream_slope, plane, slope_x, slope_y, joint_bin, square, tendency
        )
    sums = sum(square[BINS * i : BINS * i + BINS, BINS * i : BINS * i + BINS] for i in range(4))
    scale = (BINS * BINS / (total_x * total_y * levels)) ** 0.5
    row_share, col_share = BINS // stream, BINS // span
    pieces_of = sums.reshape(stream, row_share, span, col_share).transpose(0, 2, 1, 3)
    pieces_of = pieces_of.reshape(stream * span, row_share * col_share)
    received = lax.all_to_all(pieces_of, ("gx", "gy"), split_axis=0, concat_axis=0, tiled=True)
    own_sums = received.sum(0).reshape(row_share, col_share)
    return tendency, own_sums * scale


def solution(mesh):
    placed = (
        P(None, "gx", None, "gy"),
        P("gx", "gy"),
        P("gx", "gy"),
        P("gx"),
        P(),
        P("gx", None, "gy"),
    )
    return jax.shard_map(
        shards,
        mesh=mesh,
        in_specs=placed,
        out_specs=(P(None, "gx", None, "gy"), P("gx", "gy")),
        check_vma=False,
    )
```
